256 devices in a mesh: tgt: 64 (over x, z, core), sec: 4 (over y).
Axes of the slice: x: 4, y: 4, z: 8, core: 2. Of those that a mesh axis runs over, the one named last changes fastest.
Arguments:
- queries: bfloat16 [16384, 4096], P('tgt', 'sec'), may hold values from -210 to 210
- key_values: bfloat16 [2, 16384, 4096], P(None, 'tgt', 'sec'), may hold values from -6.06 to 6.06
- grad_out: bfloat16 [16384, 4096], P('tgt', 'sec'), may hold values from -192 to 192
- block_ids: int32 [128, 4], P('tgt'), may hold values from 0 to 127, as said below
- block_count: int32 [128], P('tgt'), may hold values from 1 to 4, as said below
- kv_weight: bfloat16 [2, 4096, 4096], P(None, 'tgt', 'sec'), may hold values from -0.0625 to 0.0625
Outputs:
- grad_queries: bfloat16 [16384, 4096], P('tgt', 'sec')
- grad_memory: bfloat16 [16384, 4096], P('tgt', 'sec')
The draws below stay inside these ranges and needn't reach their ends.
Inputs may be any that keep to these rules, and one draw needn't show every extreme that they name: `block_ids`: target block i, which lies in the rows of index t = i // 2 of tgt, lists only source blocks in the rows of indices t - 1, t and t + 1; its first entry is block i itself; its live entries are distinct; entries past its count repeat block i. `block_count`: every eighth block, starting at block 3, has all slots live.
All inputs are finite; a program needn't handle non-finite values.
Results may differ from the reference program's by a relative error of at most 0.013.
Values may be sent and summed in bfloat16 or wider, within the bound.
A program may use at most 128 MiB of HBM per device.

```python
import jax
import jax.numpy as jnp
from jax import lax

D = 4096
HEADS = 64
HEAD_DIM = 64
BLOCK = 128
SLOTS = 4
ROWS_DEV = 256
ROWS = 16384
N_SEC = 4


def base_pairs(key):
    width = HEADS * HEAD_DIM
    values = jnp.clip(jax.random.normal(jax.random.fold_in(key, 31), (2, ROWS, width), jnp.float32), -6.0, 6.0)
    return values


def draw_key_values(key, part):
    return base_pairs(key).astype(jnp.bfloat16)


def draw_queries(key, part):
    width = HEADS * HEAD_DIM
    drawn = jnp.clip(jax.random.normal(jax.random.fold_in(key, 32), (ROWS, width), jnp.float32), -6.0, 6.0)
    return drawn.astype(jnp.bfloat16)


def align_lists(key):
    nblocks = ROWS // BLOCK
    per_device = ROWS_DEV // BLOCK
    counts = jax.random.randint(jax.random.fold_in(key, 21), (nblocks,), 1, SLOTS + 1)
    block_pos = jnp.arange(nblocks)
    counts = jnp.where(block_pos % 8 == 3, SLOTS, counts).astype(jnp.int32)
    device_of = block_pos // per_device
    first = (device_of - 1) * per_device
    candidate = first[:, None] + jnp.arange(3 * per_device)[None, :]
    usable = (candidate >= 0) & (candidate < nblocks) & (candidate != block_pos[:, None])
    rank_keys = jax.random.randint(jax.random.fold_in(key, 22), (nblocks, 3 * per_device), 0, 1000)
    rank_keys = rank_keys * (4 * per_device) + jnp.arange(3 * per_device)[None, :]
    rank_keys = jnp.where(usable, rank_keys, 100000000)
    order = jnp.argsort(rank_keys, axis=1, stable=True)
    others = jnp.take_along_axis(candidate, order[:, :SLOTS - 1], axis=1)
    listed = jnp.concatenate([block_pos[:, None], others], axis=1)
    slot_pos = jnp.arange(SLOTS)[None, :]
    listed = jnp.where(slot_pos < counts[:, None], listed, block_pos[:, None])
    return (listed.astype(jnp.int32), counts)


def draw_block_ids(key, part):
    return align_lists(key)[0]


def draw_block_count(key, part):
    return align_lists(key)[1]


def block_scale(key, dims, shards, least, largest):
    level = 1.0
    for position, parts in shards:
        draws = jax.random.uniform(jax.random.fold_in(jax.random.fold_in(key, 6), position), (parts,), jnp.float32, least / len(shards), largest / len(shards))
        level = level * jnp.repeat(jnp.exp(draws), dims[position] // parts).reshape((-1,) + (1,) * (len(dims) - 1 - position))
    return level


def noise(key, dims, spread, limit, pieces=(), dtype=jnp.bfloat16):
    result = jax.random.normal(key, dims, jnp.float32) * spread
    if len(pieces) > 0:
        result = block_scale(key, dims, pieces, -0.22, 0.18) * result
    return jnp.clip(result, min=-limit, max=limit).astype(dtype)


def setup_inputs(seed: int = 0) -> dict:
    key_list = jax.random.split(jax.random.key(seed), 7)
    queries = draw_queries(jax.random.fold_in(key_list[6], 71), 0)
    key_values = draw_key_values(jax.random.fold_in(key_list[6], 71), 0)
    grad_out = noise(key_list[2], (ROWS, HEADS * HEAD_DIM), 32.0, 192.0, ((0, 64), (1, 4)))
    block_ids = draw_block_ids(jax.random.fold_in(key_list[6], 71), 0)
    block_count = draw_block_count(jax.random.fold_in(key_list[6], 71), 0)
    kv_weight = noise(key_list[5], (2, D, HEADS * HEAD_DIM), (2 * HEADS * HEAD_DIM) ** -0.5, 0.0625, ((1, 64), (2, 4)))
    return dict(queries=queries, key_values=key_values, grad_out=grad_out, block_ids=block_ids, block_count=block_count, kv_weight=kv_weight)


def reference(queries, key_values, grad_out, block_ids, block_count, kv_weight):
    total_rows = queries.shape[0]
    width = queries.shape[1]
    heads = width // HEAD_DIM
    nblocks = total_rows // BLOCK
    kv_blocks = key_values.reshape(2, nblocks, BLOCK, width)

    def block_step(carry, inputs):
        query_block, upstream_block, listed, count = inputs
        picked = kv_blocks[:, listed]
        key_rows = picked[0].reshape(SLOTS * BLOCK, heads, HEAD_DIM).astype(jnp.float32)
        value_rows = picked[1].reshape(SLOTS * BLOCK, heads, HEAD_DIM).astype(jnp.float32)
        query_rows = query_block.reshape(BLOCK, heads, HEAD_DIM).astype(jnp.float32)
        upstream = upstream_block.reshape(BLOCK, heads, HEAD_DIM).astype(jnp.float32)
        key_live = jnp.repeat(jnp.arange(SLOTS) < count, BLOCK)
        scores = 0.125 * jnp.einsum("qhd,khd->hqk", query_rows, key_rows)
        scores = jnp.where(key_live[None, None, :], scores, -jnp.inf)
        row_max = jnp.max(scores, axis=-1, keepdims=True)
        expo = jnp.exp(scores - row_max)
        probs = expo / jnp.sum(expo, axis=-1, keepdims=True)
        probs_half = probs.astype(jnp.bfloat16).astype(jnp.float32)
        attended = jnp.einsum("hqk,khd->qhd", probs_half, value_rows)
        delta = jnp.sum(upstream * attended, axis=-1)
        grad_probs = jnp.einsum("qhd,khd->hqk", upstream, value_rows)
        grad_scores = probs * (grad_probs - jnp.transpose(delta)[:, :, None])
        grad_half = grad_scores.astype(jnp.bfloat16).astype(jnp.float32)
        grad_query = 0.125 * jnp.einsum("hqk,khd->qhd", grad_half, key_rows)
        grad_key = 0.125 * jnp.einsum("hqk,qhd->khd", grad_half, query_rows)
        grad_value = jnp.einsum("hqk,qhd->khd", probs_half, upstream)
        pair = jnp.stack([grad_key, grad_value]).reshape(2, SLOTS, BLOCK, width)
        carry = carry.at[:, listed].add(pair)
        return carry, grad_query.reshape(BLOCK, width).astype(jnp.bfloat16)

    start = jnp.zeros((2, nblocks, BLOCK, width), jnp.float32)
    inputs = (queries.reshape(nblocks, BLOCK, width), grad_out.reshape(nblocks, BLOCK, width),
              block_ids.astype(jnp.int32), block_count.astype(jnp.int32))
    summed, grad_blocks = lax.scan(block_step, start, inputs)
    grads_half = summed.reshape(2, total_rows, width).astype(jnp.bfloat16)
    group_width = width // N_SEC
    memory = jnp.zeros((total_rows, kv_weight.shape[1]), jnp.float32)
    for group in range(N_SEC):
        left_part = grads_half[:, :, group * group_width:(group + 1) * group_width]
        right_part = kv_weight[:, :, group * group_width:(group + 1) * group_width]
        head_part = jnp.dot(left_part[0], right_part[0].T, preferred_element_type=jnp.float32)
        head_part = head_part + jnp.dot(left_part[1], right_part[1].T, preferred_element_type=jnp.float32)
        head_half = lax.optimization_barrier(head_part.astype(jnp.bfloat16))
        memory = memory + head_half.astype(jnp.float32)
    return grad_blocks.reshape(total_rows, width), memory.astype(jnp.bfloat16)
```

```python
import functools

import jax
import jax.numpy as jnp
from jax import lax
from jax.experimental import pallas as pl
from jax.experimental.pallas import tpu as pltpu
from jax.sharding import PartitionSpec as P

MESH = pl.DeviceIdType.MESH
BLOCK = 128
SLOTS = 4
EXT = 6
PAIRS = 8
NX, NZ, NY = 4, 8, 4
LEAD = 48
F32 = jnp.float32
BF16 = jnp.bfloat16


def nt(a, b):
    return lax.dot_general(a, b, (((1,), (1,)), ((), ())), preferred_element_type=F32)


def nn(a, b):
    return lax.dot_general(a, b, (((1,), (0,)), ((), ())), preferred_element_type=F32)


def tn(a, b):
    return lax.dot_general(a, b, (((0,), (0,)), ((), ())), preferred_element_type=F32)


def kernel(
    ids_ref, cnt_ref, q_ref, kv_ref, go_ref, w_ref,
    gq_ref, gm_ref,
    wg, halo, kst, ds, own, gsend, grecv, aall,
    far, relay, near, final, keep,
    zs, zr, xs, xr, hs, hr, xhs, xhr, bs, br, bhs, bhr, bzs, bzr, gs_, gr_, as_, ar_,
    fs, fr, ns, nr, ks, kr,
):
    t = lax.axis_index("tgt")
    y = lax.axis_index("sec")
    core = t % 2
    chip = t // 2
    z = chip % NZ
    x = chip // NZ

    def at(xx, zz, cc, yy):
        return {"tgt": (((xx + NX) % NX) * NZ + (zz + NZ) % NZ) * 2 + cc, "sec": (yy + NY) % NY}

    below = {"tgt": (t + 63) % 64, "sec": y}
    above = {"tgt": (t + 1) % 64, "sec": y}
    partner = {"tgt": t + 1 - 2 * core, "sec": y}
    zto = (at(x, z + 1, core, y), at(x, z - 1, core, y))
    xto = (at(x + 1, z, core, y), at(x - 1, z, core, y))

    barrier = pltpu.get_barrier_semaphore()
    peers = [below, above, *zto, *xto]
    for cc in range(2):
        peers += [at(x, z, cc, y + 1), at(x, z, cc, y - 1)]
    for peer in peers:
        pl.semaphore_signal(barrier, inc=1, device_id=peer, device_id_type=MESH)
    pl.semaphore_wait(barrier, len(peers))

    def remote(src, dst, ssem, rsem, dev):
        return pltpu.make_async_remote_copy(
            src_ref=src, dst_ref=dst, send_sem=ssem, recv_sem=rsem, device_id=dev, device_id_type=MESH
        )

    def zpiece(zz, c0, cn):
        return wg.at[pl.ds(c0, cn), x, zz, pl.ds(0, LEAD), :]

    def zcopy(way, step, half):
        zz = (z - step + NZ) % NZ if way == 0 else (z + step) % NZ
        c0, cn = (way, 1) if half else (0, 2)
        ref = zpiece(zz, c0, cn)
        return remote(ref, ref, zs.at[way, step], zr.at[way, step], zto[way])

    def zarrive(way, step, half):
        zz = (z - step - 1 + NZ) % NZ if way == 0 else (z + step + 1) % NZ
        c0, cn = (way, 1) if half else (0, 2)
        ref = zpiece(zz, c0, cn)
        remote(ref, ref, zs.at[way, step], zr.at[way, step], zto[way]).wait_recv()

    def zof(d):
        return (z + jnp.where(d % 2 == 1, NZ - (d + 1) // 2, d // 2)) % NZ

    def xpiece(xx, d, c0, cn):
        return wg.at[pl.ds(c0, cn), (xx + NX) % NX, zof(d), pl.ds(0, LEAD), :]

    def xcopy(way, d):
        ref = xpiece(x, d, 0, 2)
        return remote(ref, ref, xs.at[way, d], xr.at[way, d], xto[way])

    def xarrive(way, d):
        ref = xpiece(x - 1 + 2 * way, d, 0, 2)
        remote(ref, ref, xs.at[way, d], xr.at[way, d], xto[way]).wait_recv()

    def xhcopy(way, d):
        ref = xpiece(x - 1 + 2 * way, d, way, 1)
        return remote(ref, ref, xhs.at[way, d], xhr.at[way, d], xto[way])

    def xharrive(way, d):
        ref = xpiece(x + 2, d, way, 1)
        remote(ref, ref, xhs.at[way, d], xhr.at[way, d], xto[way]).wait_recv()

    def bpiece(xx, c0, cn):
        return wg.at[pl.ds(c0, cn), (xx + NX) % NX, z, pl.ds(LEAD, 64 - LEAD), :]

    def bcopy(way):
        ref = bpiece(x, 0, 2)
        return remote(ref, ref, bs.at[way], br.at[way], xto[way])

    def barrive(way):
        ref = bpiece(x - 1 + 2 * way, 0, 2)
        remote(ref, ref, bs.at[way], br.at[way], xto[way]).wait_recv()

    def bhcopy(way):
        ref = bpiece(x - 1 + 2 * way, way, 1)
        return remote(ref, ref, bhs.at[way], bhr.at[way], xto[way])

    def bharrive(way):
        ref = bpiece(x + 2, way, 1)
        remote(ref, ref, bhs.at[way], bhr.at[way], xto[way]).wait_recv()

    def bzpiece(zz, c0, cn):
        return wg.at[pl.ds(c0, cn), :, (zz + NZ) % NZ, pl.ds(LEAD, 64 - LEAD), :]

    def bzcopy(way, step):
        c0, cn = (way, 1) if step == 3 else (0, 2)
        ref = bzpiece(z - step if way == 0 else z + step, c0, cn)
        return remote(ref, ref, bzs.at[way, step], bzr.at[way, step], zto[way])

    def bzarrive(way, step):
        c0, cn = (way, 1) if step == 3 else (0, 2)
        ref = bzpiece(z - step - 1 if way == 0 else z + step + 1, c0, cn)
        remote(ref, ref, bzs.at[way, step], bzr.at[way, step], zto[way]).wait_recv()

    def cols(p):
        return pl.ds(pl.multiple_of(p * 128, 128), 128)

    def hcopy(side, p):
        return remote(
            kv_ref.at[:, :, :, cols(p)], halo.at[side, :, :, :, cols(p)],
            hs.at[side, p], hr.at[side, p], above if side else below,
        )

    def gcopy(side, p):
        return remote(
            gsend.at[side, :, :, :, cols(p)], grecv.at[side, :, :, :, cols(p)],
            gs_.at[side, p], gr_.at[side, p], above if side else below,
        )

    def acopy(p):
        ref = aall.at[core, :, :, :, cols(p)]
        return remote(ref, ref, as_.at[p], ar_.at[p], partner)

    def aarrive(p):
        ref = aall.at[1 - core, :, :, :, cols(p)]
        remote(ref, ref, as_.at[p], ar_.at[p], partner).wait_recv()

    def place(c):
        return pltpu.make_async_copy(w_ref.at[c], wg.at[c, x, z], ks.at[c])

    for c in range(2):
        place(c).start()
    for side in range(2):
        hcopy(side, 0).start()
    for c in range(2):
        place(c).wait()
    for way in range(2):
        zcopy(way, 0, False).start()
        bcopy(way).start()
        xcopy(way, 0).start()

    @pl.loop(1, PAIRS)
    def _(p):
        for side in range(2):
            hcopy(side, p).start()

    def step(d):
        @pl.when(d % 2 == 1)
        def _():
            k = (d - 1) // 2

            @pl.when(d < 5)
            def _():
                zarrive(0, k, False)
                zcopy(0, k + 1, False).start()

            @pl.when(d == 5)
            def _():
                zarrive(0, k, False)
                zcopy(0, 3, True).start()

            @pl.when(d == 7)
            def _():
                zarrive(0, 3, True)
                zarrive(1, 3, True)

        @pl.when(d % 2 == 0)
        def _():
            k = d // 2 - 1

            @pl.when(d < 6)
            def _():
                zarrive(1, k, False)
                zcopy(1, k + 1, False).start()

            @pl.when(d == 6)
            def _():
                zarrive(1, k, False)
                zcopy(1, 3, True).start()

        for way in range(2):
            xcopy(way, d).start()

    def forward(d):
        for way in range(2):
            xarrive(way, d)
            xhcopy(way, d).start()

    lane = lax.broadcasted_iota(jnp.int32, (BLOCK, 128), 1)
    low_lane = lane < 64
    sub = lax.broadcasted_iota(jnp.int32, (128, BLOCK), 0)
    low_sub = sub < 64
    ds[:, :, SLOTS] = jnp.zeros((2, 2, BLOCK, 128), F32)
    first = (t - 1) * 2
    zero = jnp.zeros((BLOCK, 128), BF16)

    def attend(p, i):
        rows = pl.ds(i * BLOCK, BLOCK)
        q = q_ref[rows, cols(p)] * jnp.asarray(0.125, BF16)
        g = go_ref[rows, cols(p)]
        q2 = jnp.concatenate([jnp.where(low_lane, q, zero), jnp.where(low_lane, zero, q)], axis=0)
        g2 = jnp.concatenate([jnp.where(low_lane, g, zero), jnp.where(low_lane, zero, g)], axis=0)
        places = [jnp.clip(ids_ref[i, s] - first, 0, EXT - 1) for s in range(SLOTS)]
        k = jnp.concatenate([kst[0, pos] for pos in places], axis=0)
        v = jnp.concatenate([kst[1, pos] for pos in places], axis=0)
        scores = nt(k, q2)
        gprobs = nt(v, g2)
        top = jnp.max(scores, axis=0, keepdims=True)
        expo = []
        for s in range(SLOTS):
            off = jnp.where(s < cnt_ref[i], 0.0, 1e30).astype(F32)
            expo.append(jnp.exp(scores[s * BLOCK:(s + 1) * BLOCK] - (top + off)))
        expo = jnp.concatenate(expo, axis=0)
        probs = expo * (1.0 / jnp.sum(expo, axis=0, keepdims=True))
        half = probs.astype(BF16)
        delta = jnp.sum(half.astype(F32) * gprobs, axis=0, keepdims=True)
        ghalf = (probs * (gprobs - delta)).astype(BF16)
        gk = nn(ghalf, q2)
        gv = nn(half, g2)
        for s in range(SLOTS):
            ds[i, 0, s] = gk[s * BLOCK:(s + 1) * BLOCK]
            ds[i, 1, s] = gv[s * BLOCK:(s + 1) * BLOCK]
        gqt = tn(k, ghalf)
        gqt = jnp.where(low_sub, gqt[:, :BLOCK], gqt[:, BLOCK:])
        gq_ref[rows, cols(p)] = (0.125 * jnp.transpose(gqt)).astype(BF16)

    def slot_of(i, j):
        found = jnp.int32(SLOTS)
        for s in range(SLOTS):
            hit = (ids_ref[i, s] - first == j) & (s < cnt_ref[i])
            found = jnp.where(hit, jnp.int32(s), found)
        return found

    def finish(p):
        for side in range(2):
            gcopy(side, p).wait_recv()
        total = own[:, :, :, cols(p)] + grecv[0, :, :, :, cols(p)].astype(F32)
        total = total + grecv[1, :, :, :, cols(p)].astype(F32)
        aall[core, :, :, :, cols(p)] = total.astype(BF16)
        acopy(p).start()

    @pl.loop(0, PAIRS)
    def _(p):
        @pl.when(p >= 1)
        def _():
            step(p)

        @pl.when(p == 2)
        def _():
            for way in range(2):
                barrive(way)
                bhcopy(way).start()

        @pl.when(p == 4)
        def _():
            for way in range(2):
                bharrive(way)
            for way in range(2):
                bzcopy(way, 0).start()

        for side in range(2):
            hcopy(side, p).wait_recv()
        kst[:, 0:2] = halo[1, :, :, :, cols(p)]
        kst[:, 2:4] = kv_ref[:, :, :, cols(p)]
        kst[:, 4:6] = halo[0, :, :, :, cols(p)]
        for i in range(2):
            attend(p, i)
        for j in range(EXT):
            place0, place1 = slot_of(0, j), slot_of(1, j)
            for c in range(2):
                both = ds[0, c, place0] + ds[1, c, place1]
                if j < 2:
                    gsend[0, c, j, :, cols(p)] = both.astype(BF16)
                elif j < 4:
                    own[c, j - 2, :, cols(p)] = both
                else:
                    gsend[1, c, j - 4, :, cols(p)] = both.astype(BF16)
        for side in range(2):
            gcopy(side, p).start()

        @pl.when(p >= 4)
        def _():
            finish(p - 4)
            forward(p - 4)

    @pl.loop(4, PAIRS)
    def _(p):
        finish(p)

    for step_ in range(1, 4):
        for way in range(2):
            bzarrive(way, step_ - 1)
            bzcopy(way, step_).start()
        forward(3 + step_)
    forward(7)
    for way in range(2):
        bzarrive(way, 3)

    @pl.loop(0, PAIRS)
    def _(d):
        for way in range(2):
            xharrive(way, d)
        aarrive(d)

    def fcopy(way):
        return remote(far.at[way], relay.at[way], fs.at[way], fr.at[way], at(x, z, core, y + 1 - 2 * way))

    def ncopy(way, cc):
        return remote(
            near.at[way, cc], final.at[way, core], ns.at[way, cc], nr.at[way, core],
            at(x, z, cc, y + 1 - 2 * way),
        )

    def narrive(way, k):
        remote(
            near.at[way, 0], final.at[way, k], ns.at[way, 0], nr.at[way, k], at(x, z, core, y + 1 - 2 * way)
        ).wait_recv()

    def kcopy():
        return remote(far.at[0], keep.at[core], ks.at[2], kr.at[0], partner)

    def product(dest, cc):
        total = None
        for c in range(2):
            a = aall[cc, c].reshape(2 * BLOCK, PAIRS * 128)
            w = wg[c, dest].reshape(NZ * 64, PAIRS * 128)
            part = nt(a, w)
            total = part if total is None else total + part
        return total


    for cc in range(2):
        far[cc] = product((y + 2) % NY, cc).astype(BF16)
        fcopy(cc).start()
    for way in range(2):
        dest = (y + 1 - 2 * way + NY) % NY
        near[way, 1 - way] = product(dest, 1 - way).astype(BF16)
        ncopy(way, 1 - way).start()
        total = product(dest, way)
        fcopy(way).wait_recv()
        near[way, way] = (total + relay[way].astype(F32)).astype(BF16)
        ncopy(way, way).start()
    fcopy(0).wait_send()
    fcopy(1).wait_send()
    far[0] = product(y, 1 - core).astype(BF16)
    kcopy().start()
    keep[core] = product(y, core).astype(BF16)
    for way in range(2):
        for k in range(2):
            narrive(way, k)
    remote(far.at[0], keep.at[1 - core], ks.at[2], kr.at[0], partner).wait_recv()
    low = lax.broadcasted_iota(jnp.int32, (2 * BLOCK, 128), 1) < 64
    for q in range(4):
        c = pl.ds(q * 128, 128)
        parts = []
        for k in range(2):
            parts.append(
                final[0, k, :, c].astype(F32) + final[1, k, :, c].astype(F32) + keep[k, :, c].astype(F32)
            )
        a, b = parts
        gm_ref[:, pl.ds(q * 256, 128)] = jnp.where(low, a, pltpu.roll(b, 64, 1)).astype(BF16)
        gm_ref[:, pl.ds(q * 256 + 128, 128)] = jnp.where(low, pltpu.roll(a, 64, 1), b).astype(BF16)

    for way in range(2):
        for k in range(3):
            zcopy(way, k, False).wait_send()
        zcopy(way, 3, True).wait_send()
        bcopy(way).wait_send()
        bhcopy(way).wait_send()
        for k in range(4):
            bzcopy(way, k).wait_send()
        for cc in range(2):
            ncopy(way, cc).wait_send()
    kcopy().wait_send()

    @pl.loop(0, PAIRS)
    def _(p):
        for way in range(2):
            xcopy(way, p).wait_send()
            xhcopy(way, p).wait_send()
            hcopy(way, p).wait_send()
            gcopy(way, p).wait_send()
        acopy(p).wait_send()


def per_device(queries, key_values, grad_out, block_ids, block_count, kv_weight):
    rows, width = queries.shape
    dma = pltpu.SemaphoreType.DMA
    kv = key_values.reshape(2, 2, BLOCK, width)
    vmem = pl.BlockSpec(memory_space=pltpu.VMEM)
    smem = pl.BlockSpec(memory_space=pltpu.SMEM)
    return pl.pallas_call(
        kernel,
        out_shape=(
            jax.ShapeDtypeStruct((rows, width), BF16),
            jax.ShapeDtypeStruct((rows, width), BF16),
        ),
        in_specs=[smem, smem, vmem, vmem, vmem, vmem],
        out_specs=(vmem, vmem),
        scratch_shapes=[
            pltpu.VMEM((2, NX, NZ, 64, width), BF16),
            pltpu.VMEM((2, 2, 2, BLOCK, width), BF16),
            pltpu.VMEM((2, EXT, BLOCK, 128), BF16),
            pltpu.VMEM((2, 2, SLOTS + 1, BLOCK, 128), F32),
            pltpu.VMEM((2, 2, BLOCK, width), F32),
            pltpu.VMEM((2, 2, 2, BLOCK, width), BF16),
            pltpu.VMEM((2, 2, 2, BLOCK, width), BF16),
            pltpu.VMEM((2, 2, 2, BLOCK, width), BF16),
            pltpu.VMEM((2, 2 * BLOCK, 512), BF16),
            pltpu.VMEM((2, 2 * BLOCK, 512), BF16),
            pltpu.VMEM((2, 2, 2 * BLOCK, 512), BF16),
            pltpu.VMEM((2, 2, 2 * BLOCK, 512), BF16),
            pltpu.VMEM((2, 2 * BLOCK, 512), BF16),
            dma((2, 4)), dma((2, 4)),
            dma((2, PAIRS)), dma((2, PAIRS)),
            dma((2, PAIRS)), dma((2, PAIRS)),
            dma((2, PAIRS)), dma((2, PAIRS)),
            dma((2,)), dma((2,)),
            dma((2,)), dma((2,)),
            dma((2, 4)), dma((2, 4)),
            dma((2, PAIRS)), dma((2, PAIRS)),
            dma((PAIRS,)), dma((PAIRS,)),
            dma((2,)), dma((2,)),
            dma((2, 2)), dma((2, 2)),
            dma((3,)), dma((1,)),
        ],
        compiler_params=pltpu.CompilerParams(
            collective_id=0, has_side_effects=True, vmem_limit_bytes=56 * 1024 * 1024
        ),
    )(block_ids, block_count, queries, kv, grad_out, kv_weight)


def solution(mesh):
    return jax.shard_map(
        per_device,
        mesh=mesh,
        in_specs=(
            P("tgt", "sec"),
            P(None, "tgt", "sec"),
            P("tgt", "sec"),
            P("tgt", None),
            P("tgt"),
            P(None, "tgt", "sec"),
        ),
        out_specs=(P("tgt", "sec"), P("tgt", "sec")),
        check_vma=False,
    )
```

```python
import functools

import jax
import jax.numpy as jnp
from jax import lax
from jax.experimental import pallas as pl
from jax.experimental.pallas import tpu as pltpu
from jax.sharding import PartitionSpec as P

MESH = pl.DeviceIdType.MESH
BLOCK = 128
SLOTS = 4
EXT = 6
PAIRS = 8
NX, NZ, NY = 4, 8, 4
LEAD = 48
MOVED = 5
F32 = jnp.float32
BF16 = jnp.bfloat16


def nt(a, b):
    return lax.dot_general(a, b, (((1,), (1,)), ((), ())), preferred_element_type=F32)


def nn(a, b):
    return lax.dot_general(a, b, (((1,), (0,)), ((), ())), preferred_element_type=F32)


def tn(a, b):
    return lax.dot_general(a, b, (((0,), (0,)), ((), ())), preferred_element_type=F32)


def kernel(
    ids_ref, cnt_ref, q_ref, kv_ref, go_ref, w_ref,
    gq_ref, gm_ref,
    wga, wgb, halo, kst, ds, own, gsend, grecv, aall, cur, pend,
    far_a, relay_a, near_a, final_a, cross_a, keep_a,
    far_b, relay_b, near_b, final_b, cross_b, keep_b,
    zs, zr, xs, xr, hs, hr, xhs, xhr, bs, br, bhs, bhr, bzs, bzr, gs_, gr_, as_, ar_, ps,
    fs, fr, ns, nr, ks, kr, fbs, fbr, nbs, nbr, kbs, kbr,
):
    t = lax.axis_index("tgt")
    y = lax.axis_index("sec")
    core = t % 2
    chip = t // 2
    z = chip % NZ
    x = chip // NZ

    def at(xx, zz, cc, yy):
        return {"tgt": (((xx + NX) % NX) * NZ + (zz + NZ) % NZ) * 2 + cc, "sec": (yy + NY) % NY}

    below = {"tgt": (t + 63) % 64, "sec": y}
    above = {"tgt": (t + 1) % 64, "sec": y}
    partner = {"tgt": t + 1 - 2 * core, "sec": y}
    zto = (at(x, z + 1, core, y), at(x, z - 1, core, y))
    xto = (at(x + 1, z, core, y), at(x - 1, z, core, y))

    barrier = pltpu.get_barrier_semaphore()
    peers = [below, above, *zto, *xto]
    for cc in range(2):
        peers += [at(x, z, cc, y + 1), at(x, z, cc, y - 1)]
    for peer in peers:
        pl.semaphore_signal(barrier, inc=1, device_id=peer, device_id_type=MESH)
    pl.semaphore_wait(barrier, len(peers))

    def remote(src, dst, ssem, rsem, dev):
        return pltpu.make_async_remote_copy(
            src_ref=src, dst_ref=dst, send_sem=ssem, recv_sem=rsem, device_id=dev, device_id_type=MESH
        )

    def zpiece(zz, c0, cn):
        return wga.at[pl.ds(c0, cn), x, zz]

    def zcopy(way, step, half):
        zz = (z - step + NZ) % NZ if way == 0 else (z + step) % NZ
        c0, cn = (way, 1) if half else (0, 2)
        ref = zpiece(zz, c0, cn)
        return remote(ref, ref, zs.at[way, step], zr.at[way, step], zto[way])

    def zarrive(way, step, half):
        zz = (z - step - 1 + NZ) % NZ if way == 0 else (z + step + 1) % NZ
        c0, cn = (way, 1) if half else (0, 2)
        ref = zpiece(zz, c0, cn)
        remote(ref, ref, zs.at[way, step], zr.at[way, step], zto[way]).wait_recv()

    def zof(d):
        return (z + jnp.where(d % 2 == 1, NZ - (d + 1) // 2, d // 2)) % NZ

    def xpiece(xx, d, c0, cn):
        return wga.at[pl.ds(c0, cn), (xx + NX) % NX, zof(d)]

    def xcopy(way, d):
        ref = xpiece(x, d, 0, 2)
        return remote(ref, ref, xs.at[way, d], xr.at[way, d], xto[way])

    def xarrive(way, d):
        ref = xpiece(x - 1 + 2 * way, d, 0, 2)
        remote(ref, ref, xs.at[way, d], xr.at[way, d], xto[way]).wait_recv()

    def xhcopy(way, d, whole):
        ref = xpiece(x - 1 + 2 * way, d, 0 if whole else way, 2 if whole else 1)
        return remote(ref, ref, xhs.at[way, d], xhr.at[way, d], xto[way])

    def halves(d, act):
        moved = d < MOVED
        for way in range(2):
            whole = moved & (z == (NZ - 1 if way == 0 else 0))
            none = moved & (z == (0 if way == 0 else NZ - 1))

            @pl.when(whole)
            def _():
                act(way, d, True)

            @pl.when(jnp.logical_not(whole | none))
            def _():
                act(way, d, False)

    def xharrive(way, d, whole):
        ref = xpiece(x + 2, d, 0 if whole else way, 2 if whole else 1)
        remote(ref, ref, xhs.at[way, d], xhr.at[way, d], xto[way]).wait_recv()

    def bpiece(xx, c0, cn):
        return wgb.at[pl.ds(c0, cn), (xx + NX) % NX, z]

    def bcopy(way):
        ref = bpiece(x, 0, 2)
        return remote(ref, ref, bs.at[way], br.at[way], xto[way])

    def barrive(way):
        ref = bpiece(x - 1 + 2 * way, 0, 2)
        remote(ref, ref, bs.at[way], br.at[way], xto[way]).wait_recv()

    def bhcopy(way):
        ref = bpiece(x - 1 + 2 * way, way, 1)
        return remote(ref, ref, bhs.at[way], bhr.at[way], xto[way])

    def bharrive(way):
        ref = bpiece(x + 2, way, 1)
        remote(ref, ref, bhs.at[way], bhr.at[way], xto[way]).wait_recv()

    def bzpiece(zz, c):
        return wgb.at[c, :, (zz + NZ) % NZ]

    def bzcopy(way, step, c):
        ref = bzpiece(z - step if way == 0 else z + step, c)
        return remote(ref, ref, bzs.at[way, step, c], bzr.at[way, step, c], zto[way])

    def bzarrive(way, step, c):
        ref = bzpiece(z - step - 1 if way == 0 else z + step + 1, c)
        remote(ref, ref, bzs.at[way, step, c], bzr.at[way, step, c], zto[way]).wait_recv()

    def bzforward(step):
        for c in range(2):
            for way in range(2):
                bzarrive(way, step - 1, c)
                if step < 3 or c == way:
                    bzcopy(way, step, c).start()

    def cols(p):
        return pl.ds(pl.multiple_of(p * 128, 128), 128)

    def hcopy(side, p):
        return remote(
            kv_ref.at[:, :, :, cols(p)], halo.at[side, :, :, :, cols(p)],
            hs.at[side, p], hr.at[side, p], above if side else below,
        )

    def gcopy(side, p):
        return remote(
            gsend.at[side, :, :, :, cols(p)], grecv.at[side, :, :, :, cols(p)],
            gs_.at[side, p], gr_.at[side, p], above if side else below,
        )

    def acopy(p):
        ref = aall.at[core, :, cols(p), :]
        return remote(ref, ref, as_.at[p], ar_.at[p], partner)

    def aarrive(p):
        ref = aall.at[1 - core, :, cols(p), :]
        remote(ref, ref, as_.at[p], ar_.at[p], partner).wait_recv()

    def place(c, lead):
        if lead:
            return pltpu.make_async_copy(w_ref.at[c, pl.ds(0, LEAD)], wga.at[c, x, z], ps.at[c, 0])
        return pltpu.make_async_copy(w_ref.at[c, pl.ds(LEAD, 64 - LEAD)], wgb.at[c, x, z], ps.at[c, 1])

    for c in range(2):
        place(c, True).start()
        place(c, False).start()
    for side in range(2):
        hcopy(side, 0).start()
    for c in range(2):
        place(c, True).wait()
        place(c, False).wait()
    for way in range(2):
        bcopy(way).start()
        zcopy(way, 0, False).start()
        xcopy(way, 0).start()

    @pl.loop(1, 4)
    def _(p):
        for side in range(2):
            hcopy(side, p).start()

    def step(d):
        @pl.when(d % 2 == 1)
        def _():
            k = (d - 1) // 2

            @pl.when(d < 5)
            def _():
                zarrive(0, k, False)
                zcopy(0, k + 1, False).start()

            @pl.when(d == 5)
            def _():
                zarrive(0, k, False)
                zcopy(0, 3, True).start()

            @pl.when(d == 7)
            def _():
                zarrive(0, 3, True)
                zarrive(1, 3, True)

        @pl.when(d % 2 == 0)
        def _():
            k = d // 2 - 1

            @pl.when(d < 6)
            def _():
                zarrive(1, k, False)
                zcopy(1, k + 1, False).start()

            @pl.when(d == 6)
            def _():
                zarrive(1, k, False)
                zcopy(1, 3, True).start()

        for way in range(2):
            xcopy(way, d).start()

    def forward(d):
        for way in range(2):
            xarrive(way, d)
        halves(d, lambda *a: xhcopy(*a).start())

    lane = lax.broadcasted_iota(jnp.int32, (BLOCK, 128), 1)
    low_lane = lane < 64
    sub = lax.broadcasted_iota(jnp.int32, (128, BLOCK), 0)
    low_sub = sub < 64
    ds[:, :, SLOTS] = jnp.zeros((2, 2, BLOCK, 128), F32)
    first = (t - 1) * 2
    zero = jnp.zeros((BLOCK, 128), BF16)

    def attend(p, i):
        rows = pl.ds(i * BLOCK, BLOCK)
        q = q_ref[rows, cols(p)] * jnp.asarray(0.125, BF16)
        g = go_ref[rows, cols(p)]
        q2 = jnp.concatenate([jnp.where(low_lane, q, zero), jnp.where(low_lane, zero, q)], axis=0)
        g2 = jnp.concatenate([jnp.where(low_lane, g, zero), jnp.where(low_lane, zero, g)], axis=0)
        places = [jnp.clip(ids_ref[i, s] - first, 0, EXT - 1) for s in range(SLOTS)]
        k = jnp.concatenate([kst[0, pos] for pos in places], axis=0)
        v = jnp.concatenate([kst[1, pos] for pos in places], axis=0)
        scores = nt(k, q2)
        gprobs = nt(v, g2)
        top = jnp.max(scores, axis=0, keepdims=True)
        expo = []
        for s in range(SLOTS):
            off = jnp.where(s < cnt_ref[i], 0.0, 1e30).astype(F32)
            expo.append(jnp.exp(scores[s * BLOCK:(s + 1) * BLOCK] - (top + off)))
        expo = jnp.concatenate(expo, axis=0)
        probs = expo * (1.0 / jnp.sum(expo, axis=0, keepdims=True))
        half = probs.astype(BF16)
        delta = jnp.sum(half.astype(F32) * gprobs, axis=0, keepdims=True)
        ghalf = (probs * (gprobs - delta)).astype(BF16)
        gk = nn(ghalf, q2)
        gv = nn(half, g2)
        for s in range(SLOTS):
            ds[i, 0, s] = gk[s * BLOCK:(s + 1) * BLOCK]
            ds[i, 1, s] = gv[s * BLOCK:(s + 1) * BLOCK]
        gqt = tn(k, ghalf)
        gqt = jnp.where(low_sub, gqt[:, :BLOCK], gqt[:, BLOCK:])
        gq_ref[rows, cols(p)] = (0.125 * jnp.transpose(gqt)).astype(BF16)

    def slot_of(i, j):
        found = jnp.int32(SLOTS)
        for s in range(SLOTS):
            hit = (ids_ref[i, s] - first == j) & (s < cnt_ref[i])
            found = jnp.where(hit, jnp.int32(s), found)
        return found

    def finish(p):
        for side in range(2):
            gcopy(side, p).wait_recv()
        total = own[:, :, :, cols(p)] + grecv[0, :, :, :, cols(p)].astype(F32)
        total = total + grecv[1, :, :, :, cols(p)].astype(F32)
        for c in range(2):
            aall[core, c, cols(p), :] = jnp.transpose(total[c].reshape(2 * BLOCK, 128)).astype(BF16)
        acopy(p).start()

    @pl.loop(0, PAIRS)
    def _(p):
        @pl.when(p == 1)
        def _():
            for way in range(2):
                barrive(way)
                bhcopy(way).start()

        @pl.when((p == 2) | (p == 5))
        def _():
            d = jnp.where(p == 2, 1, 3)
            step(d)
            step(d + 1)

        @pl.when(p == 2)
        def _():
            for late in range(4, PAIRS):
                for side in range(2):
                    hcopy(side, late).start()

        @pl.when(p == 6)
        def _():
            for way in range(2):
                bharrive(way)
            for c in range(2):
                for way in range(2):
                    bzcopy(way, 0, c).start()

        for side in range(2):
            hcopy(side, p).wait_recv()
        kst[:, 0:2] = halo[1, :, :, :, cols(p)]
        kst[:, 2:4] = kv_ref[:, :, :, cols(p)]
        kst[:, 4:6] = halo[0, :, :, :, cols(p)]
        for i in range(2):
            attend(p, i)
        for j in range(EXT):
            place0, place1 = slot_of(0, j), slot_of(1, j)
            for c in range(2):
                both = ds[0, c, place0] + ds[1, c, place1]
                if j < 2:
                    gsend[0, c, j, :, cols(p)] = both.astype(BF16)
                elif j < 4:
                    own[c, j - 2, :, cols(p)] = both
                else:
                    gsend[1, c, j - 4, :, cols(p)] = both.astype(BF16)
        for side in range(2):
            gcopy(side, p).start()

    step(5)
    step(6)

    @pl.loop(0, 3)
    def _(d):
        forward(d)

    step(7)
    forward(3)
    forward(4)

    @pl.loop(0, 4)
    def _(p):
        finish(p)

    bzforward(1)
    forward(5)
    forward(6)

    @pl.loop(4, PAIRS)
    def _(p):
        finish(p)

    forward(7)
    bzforward(2)

    @pl.loop(0, PAIRS)
    def _(d):
        aarrive(d)

    def side_of(way):
        return y + 1 - 2 * way

    def sums(n, work, halfs, sem, slot):
        far, relay, near, final, cross, keep = halfs
        fs, fr, ns, nr, ks, kr = sem

        def fcopy(way):
            return remote(work(far, way), work(relay, way), fs(way), fr(way), at(x, z, core, side_of(way)))

        def ncopy(way, cc):
            return remote(
                work(near, way, cc), work(final, way, core), ns(way, cc), nr(way, core),
                at(x, z, cc, side_of(way)),
            )

        def narrive(way, k):
            remote(
                work(near, way, 0), work(final, way, k), ns(way, 0), nr(way, k), at(x, z, core, side_of(way))
            ).wait_recv()

        def kcopy():
            return remote(work(cross), work(keep, core), ks(), kr(), partner)

        def karrive():
            remote(work(cross), work(keep, 1 - core), ks(), kr(), partner).wait_recv()

        def put(ref, values):
            ref[...] = values.reshape(ref.shape).astype(BF16)

        def begin(rel):
            mine = cur.at[pl.ds(0, n)]

            @pl.when(rel == 2)
            def _():
                for cc in range(2):
                    put(work(far, cc), mine[:, cc * 256:(cc + 1) * 256])
                    fcopy(cc).start()

            for way in range(2):
                @pl.when(rel == 1 + 2 * way)
                def _():
                    cc = 1 - way
                    put(work(near, way, cc), mine[:, cc * 256:(cc + 1) * 256])
                    ncopy(way, cc).start()
                    pend[slot(way), pl.ds(0, n)] = mine[:, way * 256:(way + 1) * 256]

            @pl.when(rel == 0)
            def _():
                other = pl.ds(pl.multiple_of((1 - core) * 256, 256), 256)
                here = pl.ds(pl.multiple_of(core * 256, 256), 256)
                put(work(cross), mine[:, other])
                kcopy().start()
                put(work(keep, core), mine[:, here])

        def complete(rel):
            for way in range(2):
                @pl.when(rel == 1 + 2 * way)
                def _():
                    fcopy(way).wait_recv()
                    came = work(relay, way)[...].astype(F32).reshape(n, 256)
                    put(work(near, way, way), pend[slot(way), pl.ds(0, n)] + came)
                    ncopy(way, way).start()

        def arrive():
            for way in range(2):
                for k in range(2):
                    narrive(way, k)
            karrive()

        def leave():
            for way in range(2):
                fcopy(way).wait_send()
                for cc in range(2):
                    ncopy(way, cc).wait_send()
            kcopy().wait_send()

        return begin, complete, arrive, leave

    def part_a(u):
        def work(ref, *lead):
            return ref.at[(*lead, pl.ds(2 * u, 2))]

        return sums(2 * LEAD, work, (far_a, relay_a, near_a, final_a, cross_a, keep_a), (
            lambda w: fs.at[w, u], lambda w: fr.at[w, u], lambda w, c: ns.at[w, c, u], lambda w, k: nr.at[w, k, u],
            lambda: ks.at[u], lambda: kr.at[u],
        ), lambda way: u)

    def work_b(ref, *lead):
        return ref.at[lead] if lead else ref

    part_b = sums(NZ * (64 - LEAD), work_b, (far_b, relay_b, near_b, final_b, cross_b, keep_b), (
        lambda w: fbs.at[w], lambda w: fbr.at[w], lambda w, c: nbs.at[w, c], lambda w, k: nbr.at[w, k],
        lambda: kbs.at[0], lambda: kbr.at[0],
    ), lambda way: 4 + way)

    def product(rows):
        weights = [rows(c) for c in range(2)]
        for cc in range(2):
            total = nn(weights[0], aall[cc, 0]) + nn(weights[1], aall[cc, 1])
            cur[pl.ds(0, total.shape[0]), pl.ds(cc * 256, 256)] = total

    def dest_a(i):
        e = i // 4
        return (x + jnp.where(e == 1, 1, jnp.where(e == 2, 3, jnp.where(e == 3, 2, 0)))) % NX

    @pl.loop(0, 16)
    def _(i):
        u = i % 4
        dest = dest_a(i)

        @pl.when(i >= 12)
        def _():
            halves(2 * u, xharrive)
            halves(2 * u + 1, xharrive)

        product(lambda c: jnp.concatenate([wga[c, dest, zof(2 * u)], wga[c, dest, zof(2 * u + 1)]], axis=0))

        @pl.when(i >= 4)
        def _():
            part_a(u)[1]((dest_a(i - 4) - y + NY) % NY)

        part_a(u)[0]((dest - y + NY) % NY)

        @pl.when(i == 5)
        def _():
            bzforward(3)

    for way in range(2):
        bzarrive(way, 3, way)
    for rel in (2, 1, 3, 0):
        dest = (y + rel) % NY
        product(lambda c: wgb[c, dest].reshape(NZ * (64 - LEAD), PAIRS * 128))
        part_b[0](jnp.int32(rel))

    @pl.loop(0, 4)
    def _(u):
        part_a(u)[1]((dest_a(15) - y + NY) % NY)

    for rel in (1, 3):
        part_b[1](jnp.int32(rel))
    for u in range(4):
        part_a(u)[2]()
    part_b[2]()

    @pl.loop(0, NZ)
    def _(d):
        zz = zof(d)
        rows = []
        for k in range(2):
            for final, keep, at_ in ((final_a, keep_a, d), (final_b, keep_b, zz)):
                rows.append(
                    final[0, k, at_].astype(F32) + final[1, k, at_].astype(F32) + keep[k, at_].astype(F32)
                )
        block = jnp.concatenate(rows, axis=0)
        gm_ref[:, cols(zz)] = jnp.transpose(block).astype(BF16)

    for way in range(2):
        for k in range(3):
            zcopy(way, k, False).wait_send()
        zcopy(way, 3, True).wait_send()
        bcopy(way).wait_send()
        bhcopy(way).wait_send()
        for k in range(4):
            for c in range(2):
                if k < 3 or c == way:
                    bzcopy(way, k, c).wait_send()
    for u in range(4):
        part_a(u)[3]()
    part_b[3]()

    @pl.loop(0, PAIRS)
    def _(p):
        for way in range(2):
            xcopy(way, p).wait_send()
            hcopy(way, p).wait_send()
            gcopy(way, p).wait_send()
        halves(p, lambda *a: xhcopy(*a).wait_send())
        acopy(p).wait_send()


def per_device(queries, key_values, grad_out, block_ids, block_count, kv_weight):
    rows, width = queries.shape
    dma = pltpu.SemaphoreType.DMA
    kv = key_values.reshape(2, 2, BLOCK, width)
    vmem = pl.BlockSpec(memory_space=pltpu.VMEM)
    smem = pl.BlockSpec(memory_space=pltpu.SMEM)
    return pl.pallas_call(
        kernel,
        out_shape=(
            jax.ShapeDtypeStruct((rows, width), BF16),
            jax.ShapeDtypeStruct((rows, width), BF16),
        ),
        in_specs=[smem, smem, vmem, vmem, vmem, vmem],
        out_specs=(vmem, vmem),
        scratch_shapes=[
            pltpu.VMEM((2, NX, NZ, LEAD, width), BF16),
            pltpu.VMEM((2, NX, NZ, 64 - LEAD, width), BF16),
            pltpu.VMEM((2, 2, 2, BLOCK, width), BF16),
            pltpu.VMEM((2, EXT, BLOCK, 128), BF16),
            pltpu.VMEM((2, 2, SLOTS + 1, BLOCK, 128), F32),
            pltpu.VMEM((2, 2, BLOCK, width), F32),
            pltpu.VMEM((2, 2, 2, BLOCK, width), BF16),
            pltpu.VMEM((2, 2, 2, BLOCK, width), BF16),
            pltpu.VMEM((2, 2, width, 2 * BLOCK), BF16),
            pltpu.VMEM((NZ * (64 - LEAD), 4 * BLOCK), F32),
            pltpu.VMEM((6, NZ * (64 - LEAD), 2 * BLOCK), F32),
            *[pltpu.VMEM((*lead, NZ, n, 2 * BLOCK), BF16)
              for n in (LEAD, 64 - LEAD) for lead in ((2,), (2,), (2, 2), (2, 2), (), (2,))],
            dma((2, 4)), dma((2, 4)),
            dma((2, PAIRS)), dma((2, PAIRS)),
            dma((2, PAIRS)), dma((2, PAIRS)),
            dma((2, PAIRS)), dma((2, PAIRS)),
            dma((2,)), dma((2,)),
            dma((2,)), dma((2,)),
            dma((2, 4, 2)), dma((2, 4, 2)),
            dma((2, PAIRS)), dma((2, PAIRS)),
            dma((PAIRS,)), dma((PAIRS,)),
            dma((2, 2)),
            dma((2, 4)), dma((2, 4)),
            dma((2, 2, 4)), dma((2, 2, 4)),
            dma((4,)), dma((4,)),
            dma((2,)), dma((2,)),
            dma((2, 2)), dma((2, 2)),
            dma((1,)), dma((1,)),
        ],
        compiler_params=pltpu.CompilerParams(
            collective_id=0, has_side_effects=True, vmem_limit_bytes=56 * 1024 * 1024
        ),
    )(block_ids, block_count, queries, kv, grad_out, kv_weight)


def solution(mesh):
    return jax.shard_map(
        per_device,
        mesh=mesh,
        in_specs=(
            P("tgt", "sec"),
            P(None, "tgt", "sec"),
            P("tgt", "sec"),
            P("tgt", None),
            P("tgt"),
            P(None, "tgt", "sec"),
        ),
        out_specs=(P("tgt", "sec"), P("tgt", "sec")),
        check_vma=False,
    )
```

```python
import functools

import jax
import jax.numpy as jnp
from jax import lax
from jax.experimental import pallas as pl
from jax.experimental.pallas import tpu as pltpu
from jax.sharding import PartitionSpec as P

MESH = pl.DeviceIdType.MESH
BLOCK = 128
SLOTS = 4
EXT = 6
PAIRS = 8
NX, NZ, NY = 4, 8, 4
LEAD = 48
MOVED = 6
S34 = 5
F32 = jnp.float32
BF16 = jnp.bfloat16


def nt(a, b):
    return lax.dot_general(a, b, (((1,), (1,)), ((), ())), preferred_element_type=F32)


def nn(a, b):
    return lax.dot_general(a, b, (((1,), (0,)), ((), ())), preferred_element_type=F32)


def tn(a, b):
    return lax.dot_general(a, b, (((0,), (0,)), ((), ())), preferred_element_type=F32)


def kernel(
    ids_ref, cnt_ref, q_ref, kv_ref, go_ref, w_ref,
    gq_ref, gm_ref,
    wga, wgb, halo, kst, ds, own, gsend, grecv, aall, cur, pend,
    far_a, relay_a, near_a, final_a, cross_a, keep_a,
    far_b, relay_b, near_b, final_b, cross_b, keep_b,
    zs, zr, xs, xr, hs, hr, xhs, xhr, bs, br, bhs, bhr, bzs, bzr, gs_, gr_, as_, ar_, ps,
    fs, fr, ns, nr, ks, kr, fbs, fbr, nbs, nbr, kbs, kbr,
):
    t = lax.axis_index("tgt")
    y = lax.axis_index("sec")
    core = t % 2
    chip = t // 2
    z = chip % NZ
    x = chip // NZ

    def at(xx, zz, cc, yy):
        return {"tgt": (((xx + NX) % NX) * NZ + (zz + NZ) % NZ) * 2 + cc, "sec": (yy + NY) % NY}

    below = {"tgt": (t + 63) % 64, "sec": y}
    above = {"tgt": (t + 1) % 64, "sec": y}
    partner = {"tgt": t + 1 - 2 * core, "sec": y}
    zto = (at(x, z + 1, core, y), at(x, z - 1, core, y))
    xto = (at(x + 1, z, core, y), at(x - 1, z, core, y))

    barrier = pltpu.get_barrier_semaphore()
    peers = [below, above, *zto, *xto]
    for cc in range(2):
        peers += [at(x, z, cc, y + 1), at(x, z, cc, y - 1)]
    for peer in peers:
        pl.semaphore_signal(barrier, inc=1, device_id=peer, device_id_type=MESH)
    pl.semaphore_wait(barrier, len(peers))

    def remote(src, dst, ssem, rsem, dev):
        return pltpu.make_async_remote_copy(
            src_ref=src, dst_ref=dst, send_sem=ssem, recv_sem=rsem, device_id=dev, device_id_type=MESH
        )

    def zpiece(zz, c0, cn):
        return wga.at[pl.ds(c0, cn), x, zz]

    def zcopy(way, step, half):
        zz = (z - step + NZ) % NZ if way == 0 else (z + step) % NZ
        c0, cn = (way, 1) if half else (0, 2)
        ref = zpiece(zz, c0, cn)
        return remote(ref, ref, zs.at[way, step], zr.at[way, step], zto[way])

    def zarrive(way, step, half):
        zz = (z - step - 1 + NZ) % NZ if way == 0 else (z + step + 1) % NZ
        c0, cn = (way, 1) if half else (0, 2)
        ref = zpiece(zz, c0, cn)
        remote(ref, ref, zs.at[way, step], zr.at[way, step], zto[way]).wait_recv()

    def zof(d):
        return (z + jnp.where(d % 2 == 1, NZ - (d + 1) // 2, d // 2)) % NZ

    def xpiece(xx, d, c0, cn):
        return wga.at[pl.ds(c0, cn), (xx + NX) % NX, zof(d)]

    def xcopy(way, d):
        ref = xpiece(x, d, 0, 2)
        return remote(ref, ref, xs.at[way, d], xr.at[way, d], xto[way])

    def hot(way):
        return z == (0 if way == 0 else NZ - 1)

    def xarrive(way, d):
        ref = xpiece(x - 1 + 2 * way, d, 0, 2)
        remote(ref, ref, xs.at[way, d], xr.at[way, d], xto[way]).wait_recv()

    def xhcopy(way, d, whole):
        ref = xpiece(x - 1 + 2 * way, d, 0 if whole else way, 2 if whole else 1)
        return remote(ref, ref, xhs.at[way, d], xhr.at[way, d], xto[way])

    def halves(d, act, ways=(0, 1)):
        moved = d < MOVED
        for way in ways:
            whole = moved & hot(1 - way)
            none = moved & hot(way)

            @pl.when(whole)
            def _():
                act(way, d, True)

            @pl.when(jnp.logical_not(whole | none))
            def _():
                act(way, d, False)

    def xharrive(way, d, whole):
        ref = xpiece(x + 2, d, 0 if whole else way, 2 if whole else 1)
        remote(ref, ref, xhs.at[way, d], xhr.at[way, d], xto[way]).wait_recv()

    def bpiece(xx, c0, cn):
        return wgb.at[pl.ds(c0, cn), (xx + NX) % NX, z]

    def bcopy(way):
        ref = bpiece(x, 0, 2)
        return remote(ref, ref, bs.at[way], br.at[way], xto[way])

    def barrive(way):
        ref = bpiece(x - 1 + 2 * way, 0, 2)
        remote(ref, ref, bs.at[way], br.at[way], xto[way]).wait_recv()

    def bhcopy(way):
        ref = bpiece(x - 1 + 2 * way, way, 1)
        return remote(ref, ref, bhs.at[way], bhr.at[way], xto[way])

    def bharrive(way):
        ref = bpiece(x + 2, way, 1)
        remote(ref, ref, bhs.at[way], bhr.at[way], xto[way]).wait_recv()

    def bzpiece(zz, c):
        return wgb.at[c, :, (zz + NZ) % NZ]

    def bzcopy(way, step, c):
        ref = bzpiece(z - step if way == 0 else z + step, c)
        return remote(ref, ref, bzs.at[way, step, c], bzr.at[way, step, c], zto[way])

    def bzarrive(way, step, c):
        ref = bzpiece(z - step - 1 if way == 0 else z + step + 1, c)
        remote(ref, ref, bzs.at[way, step, c], bzr.at[way, step, c], zto[way]).wait_recv()

    def bzforward(step):
        for c in range(2):
            for way in range(2):
                bzarrive(way, step - 1, c)
                if step < 3 or c == way:
                    bzcopy(way, step, c).start()

    def cols(p):
        return pl.ds(pl.multiple_of(p * 128, 128), 128)

    def hcopy(side, p):
        return remote(
            kv_ref.at[:, :, :, cols(p)], halo.at[side, :, :, :, cols(p)],
            hs.at[side, p], hr.at[side, p], above if side else below,
        )

    def gcopy(side, p):
        return remote(
            gsend.at[side, :, :, :, cols(p)], grecv.at[side, :, :, :, cols(p)],
            gs_.at[side, p], gr_.at[side, p], above if side else below,
        )

    def acopy(p):
        ref = aall.at[core, :, cols(p), :]
        return remote(ref, ref, as_.at[p], ar_.at[p], partner)

    def aarrive(p):
        ref = aall.at[1 - core, :, cols(p), :]
        remote(ref, ref, as_.at[p], ar_.at[p], partner).wait_recv()

    def place(c, lead):
        if lead:
            return pltpu.make_async_copy(w_ref.at[c, pl.ds(0, LEAD)], wga.at[c, x, z], ps.at[c, 0])
        return pltpu.make_async_copy(w_ref.at[c, pl.ds(LEAD, 64 - LEAD)], wgb.at[c, x, z], ps.at[c, 1])

    for c in range(2):
        place(c, True).start()
        place(c, False).start()
    for side in range(2):
        hcopy(side, 0).start()
    for c in range(2):
        place(c, True).wait()
        place(c, False).wait()
    for way in range(2):
        bcopy(way).start()
        zcopy(way, 0, False).start()
        xcopy(way, 0).start()

    @pl.loop(1, 6)
    def _(p):
        for side in range(2):
            hcopy(side, p).start()

    def step(d):
        @pl.when(d % 2 == 1)
        def _():
            k = (d - 1) // 2

            @pl.when(d < 5)
            def _():
                zarrive(0, k, False)
                zcopy(0, k + 1, False).start()

            @pl.when(d == 5)
            def _():
                zarrive(0, k, False)
                zcopy(0, 3, True).start()

            @pl.when(d == 7)
            def _():
                zarrive(0, 3, True)
                zarrive(1, 3, True)

        @pl.when(d % 2 == 0)
        def _():
            k = d // 2 - 1

            @pl.when(d < 6)
            def _():
                zarrive(1, k, False)
                zcopy(1, k + 1, False).start()

            @pl.when(d == 6)
            def _():
                zarrive(1, k, False)
                zcopy(1, 3, True).start()

        for way in range(2):
            xcopy(way, d).start()

    def send_half(*which):
        xhcopy(*which).start()

    def forward(d):
        for way in range(2):
            @pl.when(jnp.logical_not(hot(way)))
            def _():
                xarrive(way, d)
                halves(d, send_half, (way,))

    def forward_late(d):
        for way in range(2):
            @pl.when(hot(way))
            def _():
                xarrive(way, d)
                halves(d, send_half, (way,))

    lane = lax.broadcasted_iota(jnp.int32, (BLOCK, 128), 1)
    low_lane = lane < 64
    sub = lax.broadcasted_iota(jnp.int32, (128, BLOCK), 0)
    low_sub = sub < 64
    ds[:, :, SLOTS] = jnp.zeros((2, 2, BLOCK, 128), F32)
    first = (t - 1) * 2
    zero = jnp.zeros((BLOCK, 128), BF16)

    def attend(p, i):
        rows = pl.ds(i * BLOCK, BLOCK)
        q = q_ref[rows, cols(p)] * jnp.asarray(0.125, BF16)
        g = go_ref[rows, cols(p)]
        q2 = jnp.concatenate([jnp.where(low_lane, q, zero), jnp.where(low_lane, zero, q)], axis=0)
        g2 = jnp.concatenate([jnp.where(low_lane, g, zero), jnp.where(low_lane, zero, g)], axis=0)
        places = [jnp.clip(ids_ref[i, s] - first, 0, EXT - 1) for s in range(SLOTS)]
        k = jnp.concatenate([kst[0, pos] for pos in places], axis=0)
        v = jnp.concatenate([kst[1, pos] for pos in places], axis=0)
        scores = nt(k, q2)
        gprobs = nt(v, g2)
        top = jnp.max(scores, axis=0, keepdims=True)
        expo = []
        for s in range(SLOTS):
            off = jnp.where(s < cnt_ref[i], 0.0, 1e30).astype(F32)
            expo.append(jnp.exp(scores[s * BLOCK:(s + 1) * BLOCK] - (top + off)))
        expo = jnp.concatenate(expo, axis=0)
        probs = expo * (1.0 / jnp.sum(expo, axis=0, keepdims=True))
        half = probs.astype(BF16)
        delta = jnp.sum(half.astype(F32) * gprobs, axis=0, keepdims=True)
        ghalf = (probs * (gprobs - delta)).astype(BF16)
        gk = nn(ghalf, q2)
        gv = nn(half, g2)
        for s in range(SLOTS):
            ds[i, 0, s] = gk[s * BLOCK:(s + 1) * BLOCK]
            ds[i, 1, s] = gv[s * BLOCK:(s + 1) * BLOCK]
        gqt = tn(k, ghalf)
        gqt = jnp.where(low_sub, gqt[:, :BLOCK], gqt[:, BLOCK:])
        gq_ref[rows, cols(p)] = (0.125 * jnp.transpose(gqt)).astype(BF16)

    def slot_of(i, j):
        found = jnp.int32(SLOTS)
        for s in range(SLOTS):
            hit = (ids_ref[i, s] - first == j) & (s < cnt_ref[i])
            found = jnp.where(hit, jnp.int32(s), found)
        return found

    def finish(p):
        for side in range(2):
            gcopy(side, p).wait_recv()
        total = own[:, :, :, cols(p)] + grecv[0, :, :, :, cols(p)].astype(F32)
        total = total + grecv[1, :, :, :, cols(p)].astype(F32)
        for c in range(2):
            aall[core, c, cols(p), :] = jnp.transpose(total[c].reshape(2 * BLOCK, 128)).astype(BF16)
        acopy(p).start()

    @pl.loop(0, PAIRS)
    def _(p):
        @pl.when(p == 1)
        def _():
            for way in range(2):
                barrive(way)
                bhcopy(way).start()

        @pl.when((p == 2) | (p == S34))
        def _():
            d = jnp.where(p == 2, 1, 3)
            step(d)
            step(d + 1)

        @pl.when(p == 2)
        def _():
            for late in range(6, PAIRS):
                for side in range(2):
                    hcopy(side, late).start()

        @pl.when(p == 6)
        def _():
            for way in range(2):
                bharrive(way)

        for side in range(2):
            hcopy(side, p).wait_recv()
        kst[:, 0:2] = halo[1, :, :, :, cols(p)]
        kst[:, 2:4] = kv_ref[:, :, :, cols(p)]
        kst[:, 4:6] = halo[0, :, :, :, cols(p)]
        for i in range(2):
            attend(p, i)
        for j in range(EXT):
            place0, place1 = slot_of(0, j), slot_of(1, j)
            for c in range(2):
                both = ds[0, c, place0] + ds[1, c, place1]
                if j < 2:
                    gsend[0, c, j, :, cols(p)] = both.astype(BF16)
                elif j < 4:
                    own[c, j - 2, :, cols(p)] = both
                else:
                    gsend[1, c, j - 4, :, cols(p)] = both.astype(BF16)
    step(5)
    step(6)

    @pl.loop(0, PAIRS)
    def _(p):
        for side in range(2):
            gcopy(side, p).start()

    step(7)
    for c in range(2):
        for way in range(2):
            bzcopy(way, 0, c).start()

    @pl.loop(0, 6)
    def _(d):
        forward(d)

    @pl.loop(0, PAIRS)
    def _(p):
        finish(p)

    bzforward(1)
    forward(6)
    forward(7)

    @pl.loop(0, PAIRS)
    def _(d):
        aarrive(d)

    def side_of(way):
        return y + 1 - 2 * way

    def sums(n, work, halfs, sem, slot):
        far, relay, near, final, cross, keep = halfs
        fs, fr, ns, nr, ks, kr = sem

        def fcopy(way):
            return remote(work(far, way), work(relay, way), fs(way), fr(way), at(x, z, core, side_of(way)))

        def ncopy(way, cc):
            return remote(
                work(near, way, cc), work(final, way, core), ns(way, cc), nr(way, core),
                at(x, z, cc, side_of(way)),
            )

        def narrive(way, k):
            remote(
                work(near, way, 0), work(final, way, k), ns(way, 0), nr(way, k), at(x, z, core, side_of(way))
            ).wait_recv()

        def kcopy():
            return remote(work(cross), work(keep, core), ks(), kr(), partner)

        def karrive():
            remote(work(cross), work(keep, 1 - core), ks(), kr(), partner).wait_recv()

        def put(ref, values):
            ref[...] = values.reshape(ref.shape).astype(BF16)

        def begin(rel):
            mine = cur.at[pl.ds(0, n)]

            @pl.when(rel == 2)
            def _():
                for cc in range(2):
                    put(work(far, cc), mine[:, cc * 256:(cc + 1) * 256])
                    fcopy(cc).start()

            for way in range(2):
                @pl.when(rel == 1 + 2 * way)
                def _():
                    cc = 1 - way
                    put(work(near, way, cc), mine[:, cc * 256:(cc + 1) * 256])
                    ncopy(way, cc).start()
                    pend[slot(way), pl.ds(0, n)] = mine[:, way * 256:(way + 1) * 256]

            @pl.when(rel == 0)
            def _():
                other = pl.ds(pl.multiple_of((1 - core) * 256, 256), 256)
                here = pl.ds(pl.multiple_of(core * 256, 256), 256)
                put(work(cross), mine[:, other])
                kcopy().start()
                put(work(keep, core), mine[:, here])

        def complete(rel):
            for way in range(2):
                @pl.when(rel == 1 + 2 * way)
                def _():
                    fcopy(way).wait_recv()
                    came = work(relay, way)[...].astype(F32).reshape(n, 256)
                    put(work(near, way, way), pend[slot(way), pl.ds(0, n)] + came)
                    ncopy(way, way).start()

        def arrive():
            for way in range(2):
                for k in range(2):
                    narrive(way, k)
            karrive()

        def leave():
            for way in range(2):
                fcopy(way).wait_send()
                for cc in range(2):
                    ncopy(way, cc).wait_send()
            kcopy().wait_send()

        return begin, complete, arrive, leave

    def part_a(u):
        def work(ref, *lead):
            return ref.at[(*lead, pl.ds(2 * u, 2))]

        return sums(2 * LEAD, work, (far_a, relay_a, near_a, final_a, cross_a, keep_a), (
            lambda w: fs.at[w, u], lambda w: fr.at[w, u], lambda w, c: ns.at[w, c, u], lambda w, k: nr.at[w, k, u],
            lambda: ks.at[u], lambda: kr.at[u],
        ), lambda way: u)

    def work_b(ref, *lead):
        return ref.at[lead] if lead else ref

    part_b = sums(NZ * (64 - LEAD), work_b, (far_b, relay_b, near_b, final_b, cross_b, keep_b), (
        lambda w: fbs.at[w], lambda w: fbr.at[w], lambda w, c: nbs.at[w, c], lambda w, k: nbr.at[w, k],
        lambda: kbs.at[0], lambda: kbr.at[0],
    ), lambda way: 4 + way)

    def product(rows):
        weights = [rows(c) for c in range(2)]
        for cc in range(2):
            total = nn(weights[0], aall[cc, 0]) + nn(weights[1], aall[cc, 1])
            cur[pl.ds(0, total.shape[0]), pl.ds(cc * 256, 256)] = total

    def dest_a(i):
        e = i // 4
        return (x + jnp.where(e == 1, 1, jnp.where(e == 2, 3, jnp.where(e == 3, 2, 0)))) % NX

    @pl.loop(0, 16)
    def _(i):
        u = i % 4
        dest = dest_a(i)

        @pl.when(i == 4)
        def _():
            @pl.loop(0, PAIRS)
            def _(d):
                forward_late(d)

        @pl.when(i >= 12)
        def _():
            halves(2 * u, xharrive)
            halves(2 * u + 1, xharrive)

        product(lambda c: jnp.concatenate([wga[c, dest, zof(2 * u)], wga[c, dest, zof(2 * u + 1)]], axis=0))

        @pl.when(i >= 4)
        def _():
            part_a(u)[1]((dest_a(i - 4) - y + NY) % NY)

        part_a(u)[0]((dest - y + NY) % NY)

        for step_ in (2, 3):
            @pl.when(i == (7 if step_ == 2 else 14))
            def _():
                bzforward(step_)

    for way in range(2):
        bzarrive(way, 3, way)
    for rel in (2, 1, 3, 0):
        dest = (y + rel) % NY
        product(lambda c: wgb[c, dest].reshape(NZ * (64 - LEAD), PAIRS * 128))
        part_b[0](jnp.int32(rel))

    @pl.loop(0, 4)
    def _(u):
        part_a(u)[1]((dest_a(15) - y + NY) % NY)

    for rel in (1, 3):
        part_b[1](jnp.int32(rel))
    for u in range(4):
        part_a(u)[2]()
    part_b[2]()

    @pl.loop(0, NZ)
    def _(d):
        zz = zof(d)
        rows = []
        for k in range(2):
            for final, keep, at_ in ((final_a, keep_a, d), (final_b, keep_b, zz)):
                rows.append(
                    final[0, k, at_].astype(F32) + final[1, k, at_].astype(F32) + keep[k, at_].astype(F32)
                )
        block = jnp.concatenate(rows, axis=0)
        gm_ref[:, cols(zz)] = jnp.transpose(block).astype(BF16)

    for way in range(2):
        for k in range(3):
            zcopy(way, k, False).wait_send()
        zcopy(way, 3, True).wait_send()
        bcopy(way).wait_send()
        bhcopy(way).wait_send()
        for k in range(4):
            for c in range(2):
                if k < 3 or c == way:
                    bzcopy(way, k, c).wait_send()
    for u in range(4):
        part_a(u)[3]()
    part_b[3]()

    @pl.loop(0, PAIRS)
    def _(p):
        for way in range(2):
            xcopy(way, p).wait_send()
            hcopy(way, p).wait_send()
            gcopy(way, p).wait_send()
        halves(p, lambda *a: xhcopy(*a).wait_send())
        acopy(p).wait_send()


def per_device(queries, key_values, grad_out, block_ids, block_count, kv_weight):
    rows, width = queries.shape
    dma = pltpu.SemaphoreType.DMA
    kv = key_values.reshape(2, 2, BLOCK, width)
    vmem = pl.BlockSpec(memory_space=pltpu.VMEM)
    smem = pl.BlockSpec(memory_space=pltpu.SMEM)
    return pl.pallas_call(
        kernel,
        out_shape=(
            jax.ShapeDtypeStruct((rows, width), BF16),
            jax.ShapeDtypeStruct((rows, width), BF16),
        ),
        in_specs=[smem, smem, vmem, vmem, vmem, vmem],
        out_specs=(vmem, vmem),
        scratch_shapes=[
            pltpu.VMEM((2, NX, NZ, LEAD, width), BF16),
            pltpu.VMEM((2, NX, NZ, 64 - LEAD, width), BF16),
            pltpu.VMEM((2, 2, 2, BLOCK, width), BF16),
            pltpu.VMEM((2, EXT, BLOCK, 128), BF16),
            pltpu.VMEM((2, 2, SLOTS + 1, BLOCK, 128), F32),
            pltpu.VMEM((2, 2, BLOCK, width), F32),
            pltpu.VMEM((2, 2, 2, BLOCK, width), BF16),
            pltpu.VMEM((2, 2, 2, BLOCK, width), BF16),
            pltpu.VMEM((2, 2, width, 2 * BLOCK), BF16),
            pltpu.VMEM((NZ * (64 - LEAD), 4 * BLOCK), F32),
            pltpu.VMEM((6, NZ * (64 - LEAD), 2 * BLOCK), F32),
            *[pltpu.VMEM((*lead, NZ, n, 2 * BLOCK), BF16)
              for n in (LEAD, 64 - LEAD) for lead in ((2,), (2,), (2, 2), (2, 2), (), (2,))],
            dma((2, 4)), dma((2, 4)),
            dma((2, PAIRS)), dma((2, PAIRS)),
            dma((2, PAIRS)), dma((2, PAIRS)),
            dma((2, PAIRS)), dma((2, PAIRS)),
            dma((2,)), dma((2,)),
            dma((2,)), dma((2,)),
            dma((2, 4, 2)), dma((2, 4, 2)),
            dma((2, PAIRS)), dma((2, PAIRS)),
            dma((PAIRS,)), dma((PAIRS,)),
            dma((2, 2)),
            dma((2, 4)), dma((2, 4)),
            dma((2, 2, 4)), dma((2, 2, 4)),
            dma((4,)), dma((4,)),
            dma((2,)), dma((2,)),
            dma((2, 2)), dma((2, 2)),
            dma((1,)), dma((1,)),
        ],
        compiler_params=pltpu.CompilerParams(
            collective_id=0, has_side_effects=True, vmem_limit_bytes=56 * 1024 * 1024
        ),
    )(block_ids, block_count, queries, kv, grad_out, kv_weight)


def solution(mesh):
    return jax.shard_map(
        per_device,
        mesh=mesh,
        in_specs=(
            P("tgt", "sec"),
            P(None, "tgt", "sec"),
            P("tgt", "sec"),
            P("tgt", None),
            P("tgt"),
            P(None, "tgt", "sec"),
        ),
        out_specs=(P("tgt", "sec"), P("tgt", "sec")),
        check_vma=False,
    )
```

```python
import functools

import jax
import jax.numpy as jnp
from jax import lax
from jax.experimental import pallas as pl
from jax.experimental.pallas import tpu as pltpu
from jax.sharding import PartitionSpec as P

MESH = pl.DeviceIdType.MESH
BLOCK = 128
SLOTS = 4
EXT = 6
PAIRS = 8
NX, NZ, NY = 4, 8, 4
LEAD = 48
MOVED = 6
S34 = 5
F32 = jnp.float32
BF16 = jnp.bfloat16


def nt(a, b):
    return lax.dot_general(a, b, (((1,), (1,)), ((), ())), preferred_element_type=F32)


def nn(a, b):
    return lax.dot_general(a, b, (((1,), (0,)), ((), ())), preferred_element_type=F32)


def tn(a, b):
    return lax.dot_general(a, b, (((0,), (0,)), ((), ())), preferred_element_type=F32)


def kernel(
    ids_ref, cnt_ref, q_ref, kv_ref, go_ref, w_ref,
    gq_ref, gm_ref,
    wga, wgb, halo, kst, ds, own, gsend, grecv, aall, cur, pend,
    far_a, relay_a, near_a, final_a, cross_a, keep_a,
    far_b, relay_b, near_b, final_b, cross_b, keep_b,
    zs, zr, xs, xr, hs, hr, xhs, xhr, bs, br, bhs, bhr, bzs, bzr, gs_, gr_, as_, ar_, ps,
    fs, fr, ns, nr, ks, kr, fbs, fbr, nbs, nbr, kbs, kbr,
):
    t = lax.axis_index("tgt")
    y = lax.axis_index("sec")
    core = t % 2
    chip = t // 2
    z = chip % NZ
    x = chip // NZ

    def at(xx, zz, cc, yy):
        return {"tgt": (((xx + NX) % NX) * NZ + (zz + NZ) % NZ) * 2 + cc, "sec": (yy + NY) % NY}

    below = {"tgt": (t + 63) % 64, "sec": y}
    above = {"tgt": (t + 1) % 64, "sec": y}
    partner = {"tgt": t + 1 - 2 * core, "sec": y}
    zto = (at(x, z + 1, core, y), at(x, z - 1, core, y))
    xto = (at(x + 1, z, core, y), at(x - 1, z, core, y))

    barrier = pltpu.get_barrier_semaphore()
    peers = [below, above, *zto, *xto]
    for cc in range(2):
        peers += [at(x, z, cc, y + 1), at(x, z, cc, y - 1)]
    for peer in peers:
        pl.semaphore_signal(barrier, inc=1, device_id=peer, device_id_type=MESH)
    pl.semaphore_wait(barrier, len(peers))

    def remote(src, dst, ssem, rsem, dev):
        return pltpu.make_async_remote_copy(
            src_ref=src, dst_ref=dst, send_sem=ssem, recv_sem=rsem, device_id=dev, device_id_type=MESH
        )

    def zpiece(zz, c0, cn):
        return wga.at[pl.ds(c0, cn), x, zz]

    def zcopy(way, step, half):
        zz = (z - step + NZ) % NZ if way == 0 else (z + step) % NZ
        c0, cn = (way, 1) if half else (0, 2)
        ref = zpiece(zz, c0, cn)
        return remote(ref, ref, zs.at[way, step], zr.at[way, step], zto[way])

    def zarrive(way, step, half):
        zz = (z - step - 1 + NZ) % NZ if way == 0 else (z + step + 1) % NZ
        c0, cn = (way, 1) if half else (0, 2)
        ref = zpiece(zz, c0, cn)
        remote(ref, ref, zs.at[way, step], zr.at[way, step], zto[way]).wait_recv()

    def zof(d):
        return (z + jnp.where(d % 2 == 1, NZ - (d + 1) // 2, d // 2)) % NZ

    def xpiece(xx, d, c0, cn):
        return wga.at[pl.ds(c0, cn), (xx + NX) % NX, zof(d)]

    def xcopy(way, d):
        ref = xpiece(x, d, 0, 2)
        return remote(ref, ref, xs.at[way, d], xr.at[way, d], xto[way])

    def hot(way):
        return z == (0 if way == 0 else NZ - 1)

    def xarrive(way, d):
        ref = xpiece(x - 1 + 2 * way, d, 0, 2)
        remote(ref, ref, xs.at[way, d], xr.at[way, d], xto[way]).wait_recv()

    def xhcopy(way, d, whole):
        ref = xpiece(x - 1 + 2 * way, d, 0 if whole else way, 2 if whole else 1)
        return remote(ref, ref, xhs.at[way, d], xhr.at[way, d], xto[way])

    def halves(d, act, ways=(0, 1)):
        moved = d < MOVED
        for way in ways:
            whole = moved & hot(1 - way)
            none = moved & hot(way)

            @pl.when(whole)
            def _():
                act(way, d, True)

            @pl.when(jnp.logical_not(whole | none))
            def _():
                act(way, d, False)

    def xharrive(way, d, whole):
        ref = xpiece(x + 2, d, 0 if whole else way, 2 if whole else 1)
        remote(ref, ref, xhs.at[way, d], xhr.at[way, d], xto[way]).wait_recv()

    def bpiece(xx, c0, cn):
        return wgb.at[pl.ds(c0, cn), (xx + NX) % NX, z]

    def bcopy(way):
        ref = bpiece(x, 0, 2)
        return remote(ref, ref, bs.at[way], br.at[way], xto[way])

    def barrive(way):
        ref = bpiece(x - 1 + 2 * way, 0, 2)
        remote(ref, ref, bs.at[way], br.at[way], xto[way]).wait_recv()

    def bhcopy(way):
        ref = bpiece(x - 1 + 2 * way, way, 1)
        return remote(ref, ref, bhs.at[way], bhr.at[way], xto[way])

    def bharrive(way):
        ref = bpiece(x + 2, way, 1)
        remote(ref, ref, bhs.at[way], bhr.at[way], xto[way]).wait_recv()

    def bzpiece(zz, c):
        return wgb.at[c, :, (zz + NZ) % NZ]

    def bzcopy(way, step, c):
        ref = bzpiece(z - step if way == 0 else z + step, c)
        return remote(ref, ref, bzs.at[way, step, c], bzr.at[way, step, c], zto[way])

    def bzarrive(way, step, c):
        ref = bzpiece(z - step - 1 if way == 0 else z + step + 1, c)
        remote(ref, ref, bzs.at[way, step, c], bzr.at[way, step, c], zto[way]).wait_recv()

    def bzforward(step):
        for c in range(2):
            for way in range(2):
                bzarrive(way, step - 1, c)
                if step < 3 or c == way:
                    bzcopy(way, step, c).start()

    def cols(p):
        return pl.ds(pl.multiple_of(p * 128, 128), 128)

    def hcopy(side, p):
        return remote(
            kv_ref.at[:, :, :, cols(p)], halo.at[side, :, :, :, cols(p)],
            hs.at[side, p], hr.at[side, p], above if side else below,
        )

    def gcopy(side, p):
        return remote(
            gsend.at[side, :, :, :, cols(p)], grecv.at[side, :, :, :, cols(p)],
            gs_.at[side, p], gr_.at[side, p], above if side else below,
        )

    def acopy(p):
        ref = aall.at[core, :, cols(p), :]
        return remote(ref, ref, as_.at[p], ar_.at[p], partner)

    def aarrive(p):
        ref = aall.at[1 - core, :, cols(p), :]
        remote(ref, ref, as_.at[p], ar_.at[p], partner).wait_recv()

    def place(c, lead):
        if lead:
            return pltpu.make_async_copy(w_ref.at[c, pl.ds(0, LEAD)], wga.at[c, x, z], ps.at[c, 0])
        return pltpu.make_async_copy(w_ref.at[c, pl.ds(LEAD, 64 - LEAD)], wgb.at[c, x, z], ps.at[c, 1])

    for c in range(2):
        place(c, True).start()
        place(c, False).start()
    for side in range(2):
        hcopy(side, 0).start()
    for c in range(2):
        place(c, True).wait()
        place(c, False).wait()
    for way in range(2):
        bcopy(way).start()
        zcopy(way, 0, False).start()
        xcopy(way, 0).start()

    @pl.loop(1, 6)
    def _(p):
        for side in range(2):
            hcopy(side, p).start()

    def step(d):
        @pl.when(d % 2 == 1)
        def _():
            k = (d - 1) // 2

            @pl.when(d < 5)
            def _():
                zarrive(0, k, False)
                zcopy(0, k + 1, False).start()

            @pl.when(d == 5)
            def _():
                zarrive(0, k, False)
                zcopy(0, 3, True).start()

            @pl.when(d == 7)
            def _():
                zarrive(0, 3, True)
                zarrive(1, 3, True)

        @pl.when(d % 2 == 0)
        def _():
            k = d // 2 - 1

            @pl.when(d < 6)
            def _():
                zarrive(1, k, False)
                zcopy(1, k + 1, False).start()

            @pl.when(d == 6)
            def _():
                zarrive(1, k, False)
                zcopy(1, 3, True).start()

        for way in range(2):
            xcopy(way, d).start()

    def send_half(*which):
        xhcopy(*which).start()

    def forward(d):
        for way in range(2):
            @pl.when(jnp.logical_not(hot(way)))
            def _():
                xarrive(way, d)
                halves(d, send_half, (way,))

    def forward_late(d):
        for way in range(2):
            @pl.when(hot(way))
            def _():
                xarrive(way, d)
                halves(d, send_half, (way,))

    lane = lax.broadcasted_iota(jnp.int32, (BLOCK, 128), 1)
    low_lane = lane < 64
    sub = lax.broadcasted_iota(jnp.int32, (128, BLOCK), 0)
    low_sub = sub < 64
    ds[:, :, SLOTS] = jnp.zeros((2, 2, BLOCK, 128), F32)
    first = (t - 1) * 2
    zero = jnp.zeros((BLOCK, 128), BF16)

    def attend(p, i):
        rows = pl.ds(i * BLOCK, BLOCK)
        q = q_ref[rows, cols(p)] * jnp.asarray(0.125, BF16)
        g = go_ref[rows, cols(p)]
        q2 = jnp.concatenate([jnp.where(low_lane, q, zero), jnp.where(low_lane, zero, q)], axis=0)
        g2 = jnp.concatenate([jnp.where(low_lane, g, zero), jnp.where(low_lane, zero, g)], axis=0)
        places = [jnp.clip(ids_ref[i, s] - first, 0, EXT - 1) for s in range(SLOTS)]
        k = jnp.concatenate([kst[0, pos] for pos in places], axis=0)
        v = jnp.concatenate([kst[1, pos] for pos in places], axis=0)
        scores = nt(k, q2)
        gprobs = nt(v, g2)
        top = jnp.max(scores, axis=0, keepdims=True)
        expo = []
        for s in range(SLOTS):
            off = jnp.where(s < cnt_ref[i], 0.0, 1e30).astype(F32)
            expo.append(jnp.exp(scores[s * BLOCK:(s + 1) * BLOCK] - (top + off)))
        expo = jnp.concatenate(expo, axis=0)
        probs = expo * (1.0 / jnp.sum(expo, axis=0, keepdims=True))
        half = probs.astype(BF16)
        delta = jnp.sum(half.astype(F32) * gprobs, axis=0, keepdims=True)
        ghalf = (probs * (gprobs - delta)).astype(BF16)
        gk = nn(ghalf, q2)
        gv = nn(half, g2)
        for s in range(SLOTS):
            ds[i, 0, s] = gk[s * BLOCK:(s + 1) * BLOCK]
            ds[i, 1, s] = gv[s * BLOCK:(s + 1) * BLOCK]
        gqt = tn(k, ghalf)
        gqt = jnp.where(low_sub, gqt[:, :BLOCK], gqt[:, BLOCK:])
        gq_ref[rows, cols(p)] = (0.125 * jnp.transpose(gqt)).astype(BF16)

    def slot_of(i, j):
        found = jnp.int32(SLOTS)
        for s in range(SLOTS):
            hit = (ids_ref[i, s] - first == j) & (s < cnt_ref[i])
            found = jnp.where(hit, jnp.int32(s), found)
        return found

    def finish(p):
        for side in range(2):
            gcopy(side, p).wait_recv()
        total = own[:, :, :, cols(p)] + grecv[0, :, :, :, cols(p)].astype(F32)
        total = total + grecv[1, :, :, :, cols(p)].astype(F32)
        for c in range(2):
            aall[core, c, cols(p), :] = jnp.transpose(total[c].reshape(2 * BLOCK, 128)).astype(BF16)
        acopy(p).start()

    @pl.loop(0, PAIRS)
    def _(p):
        @pl.when(p == 1)
        def _():
            for way in range(2):
                barrive(way)
                bhcopy(way).start()

        @pl.when((p == 2) | (p == S34))
        def _():
            d = jnp.where(p == 2, 1, 3)
            step(d)
            step(d + 1)

        @pl.when(p == 2)
        def _():
            for late in range(6, PAIRS):
                for side in range(2):
                    hcopy(side, late).start()

        @pl.when(p == 6)
        def _():
            for way in range(2):
                bharrive(way)

        for side in range(2):
            hcopy(side, p).wait_recv()
        kst[:, 0:2] = halo[1, :, :, :, cols(p)]
        kst[:, 2:4] = kv_ref[:, :, :, cols(p)]
        kst[:, 4:6] = halo[0, :, :, :, cols(p)]
        for i in range(2):
            attend(p, i)
        for j in range(EXT):
            place0, place1 = slot_of(0, j), slot_of(1, j)
            for c in range(2):
                both = ds[0, c, place0] + ds[1, c, place1]
                if j < 2:
                    gsend[0, c, j, :, cols(p)] = both.astype(BF16)
                elif j < 4:
                    own[c, j - 2, :, cols(p)] = both
                else:
                    gsend[1, c, j - 4, :, cols(p)] = both.astype(BF16)
    step(5)
    step(6)

    @pl.loop(0, PAIRS)
    def _(p):
        for side in range(2):
            gcopy(side, p).start()

    step(7)
    for c in range(2):
        for way in range(2):
            bzcopy(way, 0, c).start()

    @pl.loop(0, 6)
    def _(d):
        forward(d)

    @pl.loop(0, PAIRS)
    def _(p):
        finish(p)

    bzforward(1)
    forward(6)
    forward(7)

    @pl.loop(0, PAIRS)
    def _(d):
        aarrive(d)

    def side_of(way):
        return y + 1 - 2 * way

    def sums(n, work, halfs, sem, slot):
        far, relay, near, final, cross, keep = halfs
        fs, fr, ns, nr, ks, kr = sem

        def fcopy(way):
            return remote(work(far, way), work(relay, way), fs(way), fr(way), at(x, z, core, side_of(way)))

        def ncopy(way, cc):
            return remote(
                work(near, way, cc), work(final, way, core), ns(way, cc), nr(way, core),
                at(x, z, cc, side_of(way)),
            )

        def narrive(way, k):
            remote(
                work(near, way, 0), work(final, way, k), ns(way, 0), nr(way, k), at(x, z, core, side_of(way))
            ).wait_recv()

        def kcopy():
            return remote(work(cross), work(keep, core), ks(), kr(), partner)

        def karrive():
            remote(work(cross), work(keep, 1 - core), ks(), kr(), partner).wait_recv()

        def put(ref, values):
            ref[...] = values.reshape(ref.shape).astype(BF16)

        def begin(rel):
            mine = cur.at[pl.ds(0, n)]

            @pl.when(rel == 2)
            def _():
                for cc in range(2):
                    put(work(far, cc), mine[:, cc * 256:(cc + 1) * 256])
                    fcopy(cc).start()

            for way in range(2):
                @pl.when(rel == 1 + 2 * way)
                def _():
                    cc = 1 - way
                    put(work(near, way, cc), mine[:, cc * 256:(cc + 1) * 256])
                    ncopy(way, cc).start()
                    pend[slot(way), pl.ds(0, n)] = mine[:, way * 256:(way + 1) * 256]

            @pl.when(rel == 0)
            def _():
                other = pl.ds(pl.multiple_of((1 - core) * 256, 256), 256)
                here = pl.ds(pl.multiple_of(core * 256, 256), 256)
                put(work(cross), mine[:, other])
                kcopy().start()
                put(work(keep, core), mine[:, here])

        def complete(rel):
            for way in range(2):
                @pl.when(rel == 1 + 2 * way)
                def _():
                    fcopy(way).wait_recv()
                    came = work(relay, way)[...].astype(F32).reshape(n, 256)
                    put(work(near, way, way), pend[slot(way), pl.ds(0, n)] + came)
                    ncopy(way, way).start()

        def arrive():
            for way in range(2):
                for k in range(2):
                    narrive(way, k)
            karrive()

        def leave():
            for way in range(2):
                fcopy(way).wait_send()
                for cc in range(2):
                    ncopy(way, cc).wait_send()
            kcopy().wait_send()

        return begin, complete, arrive, leave

    def part_a(u):
        def work(ref, *lead):
            return ref.at[(*lead, pl.ds(2 * u, 2))]

        return sums(2 * LEAD, work, (far_a, relay_a, near_a, final_a, cross_a, keep_a), (
            lambda w: fs.at[w, u], lambda w: fr.at[w, u], lambda w, c: ns.at[w, c, u], lambda w, k: nr.at[w, k, u],
            lambda: ks.at[u], lambda: kr.at[u],
        ), lambda way: u)

    def work_b(ref, *lead):
        return ref.at[lead] if lead else ref

    part_b = sums(NZ * (64 - LEAD), work_b, (far_b, relay_b, near_b, final_b, cross_b, keep_b), (
        lambda w: fbs.at[w], lambda w: fbr.at[w], lambda w, c: nbs.at[w, c], lambda w, k: nbr.at[w, k],
        lambda: kbs.at[0], lambda: kbr.at[0],
    ), lambda way: 4 + way)

    def product(rows):
        weights = [rows(c) for c in range(2)]
        for cc in range(2):
            total = nn(weights[0], aall[cc, 0]) + nn(weights[1], aall[cc, 1])
            cur[pl.ds(0, total.shape[0]), pl.ds(cc * 256, 256)] = total

    def dest_a(i):
        e = i // 4
        swap = z == NZ - 1
        one, two = jnp.where(swap, 3, 1), jnp.where(swap, 1, 3)
        return (x + jnp.where(e == 1, one, jnp.where(e == 2, two, jnp.where(e == 3, 2, 0)))) % NX

    @pl.loop(0, 16)
    def _(i):
        u = i % 4
        dest = dest_a(i)

        @pl.when(i == 8)
        def _():
            @pl.loop(0, PAIRS)
            def _(d):
                forward_late(d)

        @pl.when(i >= 12)
        def _():
            halves(2 * u, xharrive)
            halves(2 * u + 1, xharrive)

        product(lambda c: jnp.concatenate([wga[c, dest, zof(2 * u)], wga[c, dest, zof(2 * u + 1)]], axis=0))

        @pl.when(i >= 4)
        def _():
            part_a(u)[1]((dest_a(i - 4) - y + NY) % NY)

        part_a(u)[0]((dest - y + NY) % NY)

        for step_ in (2, 3):
            @pl.when(i == (7 if step_ == 2 else 14))
            def _():
                bzforward(step_)

    for way in range(2):
        bzarrive(way, 3, way)
    for rel in (2, 1, 3, 0):
        dest = (y + rel) % NY
        product(lambda c: wgb[c, dest].reshape(NZ * (64 - LEAD), PAIRS * 128))
        part_b[0](jnp.int32(rel))

    @pl.loop(0, 4)
    def _(u):
        part_a(u)[1]((dest_a(15) - y + NY) % NY)

    for rel in (1, 3):
        part_b[1](jnp.int32(rel))
    for u in range(4):
        part_a(u)[2]()
    part_b[2]()

    @pl.loop(0, NZ)
    def _(d):
        zz = zof(d)
        rows = []
        for k in range(2):
            for final, keep, at_ in ((final_a, keep_a, d), (final_b, keep_b, zz)):
                rows.append(
                    final[0, k, at_].astype(F32) + final[1, k, at_].astype(F32) + keep[k, at_].astype(F32)
                )
        block = jnp.concatenate(rows, axis=0)
        gm_ref[:, cols(zz)] = jnp.transpose(block).astype(BF16)

    for way in range(2):
        for k in range(3):
            zcopy(way, k, False).wait_send()
        zcopy(way, 3, True).wait_send()
        bcopy(way).wait_send()
        bhcopy(way).wait_send()
        for k in range(4):
            for c in range(2):
                if k < 3 or c == way:
                    bzcopy(way, k, c).wait_send()
    for u in range(4):
        part_a(u)[3]()
    part_b[3]()

    @pl.loop(0, PAIRS)
    def _(p):
        for way in range(2):
            xcopy(way, p).wait_send()
            hcopy(way, p).wait_send()
            gcopy(way, p).wait_send()
        halves(p, lambda *a: xhcopy(*a).wait_send())
        acopy(p).wait_send()


def per_device(queries, key_values, grad_out, block_ids, block_count, kv_weight):
    rows, width = queries.shape
    dma = pltpu.SemaphoreType.DMA
    kv = key_values.reshape(2, 2, BLOCK, width)
    vmem = pl.BlockSpec(memory_space=pltpu.VMEM)
    smem = pl.BlockSpec(memory_space=pltpu.SMEM)
    return pl.pallas_call(
        kernel,
        out_shape=(
            jax.ShapeDtypeStruct((rows, width), BF16),
            jax.ShapeDtypeStruct((rows, width), BF16),
        ),
        in_specs=[smem, smem, vmem, vmem, vmem, vmem],
        out_specs=(vmem, vmem),
        scratch_shapes=[
            pltpu.VMEM((2, NX, NZ, LEAD, width), BF16),
            pltpu.VMEM((2, NX, NZ, 64 - LEAD, width), BF16),
            pltpu.VMEM((2, 2, 2, BLOCK, width), BF16),
            pltpu.VMEM((2, EXT, BLOCK, 128), BF16),
            pltpu.VMEM((2, 2, SLOTS + 1, BLOCK, 128), F32),
            pltpu.VMEM((2, 2, BLOCK, width), F32),
            pltpu.VMEM((2, 2, 2, BLOCK, width), BF16),
            pltpu.VMEM((2, 2, 2, BLOCK, width), BF16),
            pltpu.VMEM((2, 2, width, 2 * BLOCK), BF16),
            pltpu.VMEM((NZ * (64 - LEAD), 4 * BLOCK), F32),
            pltpu.VMEM((6, NZ * (64 - LEAD), 2 * BLOCK), F32),
            *[pltpu.VMEM((*lead, NZ, n, 2 * BLOCK), BF16)
              for n in (LEAD, 64 - LEAD) for lead in ((2,), (2,), (2, 2), (2, 2), (), (2,))],
            dma((2, 4)), dma((2, 4)),
            dma((2, PAIRS)), dma((2, PAIRS)),
            dma((2, PAIRS)), dma((2, PAIRS)),
            dma((2, PAIRS)), dma((2, PAIRS)),
            dma((2,)), dma((2,)),
            dma((2,)), dma((2,)),
            dma((2, 4, 2)), dma((2, 4, 2)),
            dma((2, PAIRS)), dma((2, PAIRS)),
            dma((PAIRS,)), dma((PAIRS,)),
            dma((2, 2)),
            dma((2, 4)), dma((2, 4)),
            dma((2, 2, 4)), dma((2, 2, 4)),
            dma((4,)), dma((4,)),
            dma((2,)), dma((2,)),
            dma((2, 2)), dma((2, 2)),
            dma((1,)), dma((1,)),
        ],
        compiler_params=pltpu.CompilerParams(
            collective_id=0, has_side_effects=True, vmem_limit_bytes=56 * 1024 * 1024
        ),
    )(block_ids, block_count, queries, kv, grad_out, kv_weight)


def solution(mesh):
    return jax.shard_map(
        per_device,
        mesh=mesh,
        in_specs=(
            P("tgt", "sec"),
            P(None, "tgt", "sec"),
            P("tgt", "sec"),
            P("tgt", None),
            P("tgt"),
            P(None, "tgt", "sec"),
        ),
        out_specs=(P("tgt", "sec"), P("tgt", "sec")),
        check_vma=False,
    )
```
